512 devices in a mesh: sx: 4 (over y), sy: 8 (over z_lo, core), sz: 16 (over x, z_hi).
Axes of the slice: x: 4, y: 4, z: 16 (z_hi: 4, z_lo: 4; z = z_hi * 4 + z_lo), core: 2. Of those that a mesh axis runs over, the one named last changes fastest.
Arguments:
- density: bfloat16 [4, 32, 64, 256], P(None, 'sx', 'sy', 'sz'), may hold values from -6 to 6
- conv1_weight: bfloat16 [32, 3, 3, 3, 4], replicated, may hold values from -0.625 to 0.625
- conv1_bias: float32 [32], replicated, may hold values from -3 to 3
- conv1_probe: bfloat16 [32, 3, 3, 3, 4], replicated, may hold values from -0.625 to 0.625
- conv2_weight: bfloat16 [32, 3, 3, 3, 32], replicated, may hold values from -0.21875 to 0.21875
- conv2_bias: float32 [32], replicated, may hold values from -3 to 3
- conv2_probe: bfloat16 [32, 3, 3, 3, 32], replicated, may hold values from -0.21875 to 0.21875
- lift_weight: bfloat16 [256, 4, 4, 4, 32], replicated, may hold values from -0.125 to 0.125
- lift_bias: float32 [256], replicated, may hold values from -3 to 3
- lift_probe: bfloat16 [256, 4, 4, 4, 32], replicated, may hold values from -0.125 to 0.125
- conv3_weight: bfloat16 [256, 3, 3, 3, 256], P(None, None, None, None, ('sx', 'sy')), may hold values from -0.125 to 0.125
- conv3_bias: float32 [256], P(('sx', 'sy')), may hold values from -3 to 3
- conv3_probe: bfloat16 [256, 3, 3, 3, 256], P(None, None, None, None, ('sx', 'sy')), may hold values from -0.125 to 0.125
Outputs:
- features: bfloat16 [256, 8, 16, 64], P(('sx', 'sy'), None, None, 'sz')
- tangent: bfloat16 [256, 8, 16, 64], P(('sx', 'sy'), None, None, 'sz')
The draws below stay inside these ranges and needn't reach their ends.
All inputs are finite; a program needn't handle non-finite values.
Results may differ from the reference program's by a relative error of at most 0.013.
Values may be sent and summed in bfloat16 or wider, within the bound.
No kernel may reach another device: no remote copies, remote signals or barrier semaphores. Data moves between devices by JAX's collectives and lax.ppermute only.
A program may use at most 64 MiB of HBM per device.

```python
import jax
import jax.numpy as jnp
from jax import lax

CIN = 4
C1 = 32
C3 = 256
NX = 32
NY = 64
NZ = 256


def with_spikes(entries, rng, source, target, shards_of, factor):
    def block_of(axis_at):
        return (jnp.arange(entries.shape[axis_at]) // (entries.shape[axis_at] // shards_of)).reshape((-1,) + (1,) * (entries.ndim - 1 - axis_at))

    near = jax.random.permutation(rng, shards_of)[block_of(target)]
    far = (block_of(target) + shards_of // 2) % shards_of
    return jnp.where((block_of(source) == near) | (block_of(source) == far), factor * entries, entries)


def level_of(own_key, dims, shards, low, largest):
    level, own = 1.0, jax.random.fold_in(own_key, 6)
    for position, blocks in shards:
        steps = jnp.exp(jax.random.uniform(jax.random.fold_in(own, position), (blocks,), jnp.float32, low / len(shards), largest / len(shards)))
        level = level * jnp.repeat(steps, dims[position] // blocks).reshape([-1 if axis == position else 1 for axis in range(len(dims))])
    return level


def centred(stream_key, extent, width, bound, cuts=(), held_as=jnp.bfloat16):
    factor_of = level_of(stream_key, extent, cuts, -0.22, 0.18) if cuts else 1.0
    array = jax.random.normal(stream_key, extent, jnp.float32) * width * factor_of
    return jnp.minimum(jnp.maximum(array, -bound), bound).astype(held_as)


def heavy_noise(stream_key, dims, width, most, pieces, heavy, held_as=jnp.bfloat16):
    values = width * jax.random.normal(stream_key, dims, jnp.float32)
    if pieces:
        values = values * level_of(stream_key, dims, pieces, -0.22, 0.18)
    return jnp.clip(with_spikes(values, jax.random.fold_in(stream_key, 3), *heavy), -most, most).astype(held_as)


def setup_inputs(seed: int = 0) -> dict:
    streams_of = jax.random.split(jax.random.key(seed), 14)
    density = centred(streams_of[0], (CIN, NX, NY, NZ), 1.0, 6.0, ((1, 4), (2, 8), (3, 16)))
    conv1_weight = centred(streams_of[1], (C1, 3, 3, 3, CIN), (27 * CIN) ** -0.5, 0.625)
    conv1_bias = centred(streams_of[2], (C1,), 0.5, 3.0, (), jnp.float32)
    conv1_probe = centred(streams_of[3], (C1, 3, 3, 3, CIN), (27 * CIN) ** -0.5, 0.625)
    conv2_weight = centred(streams_of[4], (C1, 3, 3, 3, C1), (27 * C1) ** -0.5, 0.21875)
    conv2_bias = centred(streams_of[5], (C1,), 0.5, 3.0, (), jnp.float32)
    conv2_probe = centred(streams_of[6], (C1, 3, 3, 3, C1), (27 * C1) ** -0.5, 0.21875)
    lift_weight = centred(streams_of[7], (C3, 4, 4, 4, C1), (64 * C1) ** -0.5, 0.125)
    lift_bias = centred(streams_of[8], (C3,), 0.5, 3.0, (), jnp.float32)
    lift_probe = centred(streams_of[9], (C3, 4, 4, 4, C1), (64 * C1) ** -0.5, 0.125)
    conv3_weight = heavy_noise(streams_of[10], (C3, 3, 3, 3, C3), (27 * C3) ** -0.5, 0.125, ((4, 32),), (4, 0, 32, 2.75))
    conv3_bias = centred(streams_of[11], (C3,), 0.5, 3.0, ((0, 32),), jnp.float32)
    conv3_probe = heavy_noise(streams_of[12], (C3, 3, 3, 3, C3), (27 * C3) ** -0.5, 0.125, ((4, 32),), (4, 0, 32, 2.75))
    return {"density": density, "conv1_weight": conv1_weight, "conv1_bias": conv1_bias, "conv1_probe": conv1_probe, "conv2_weight": conv2_weight, "conv2_bias": conv2_bias, "conv2_probe": conv2_probe, "lift_weight": lift_weight, "lift_bias": lift_bias, "lift_probe": lift_probe, "conv3_weight": conv3_weight, "conv3_bias": conv3_bias, "conv3_probe": conv3_probe}


def swish_pair(preact, direction):
    sigmoid_value = jax.nn.sigmoid(preact)
    derivative = sigmoid_value * (1.0 + preact * (1.0 - sigmoid_value))
    return preact * sigmoid_value, derivative * direction


def convolve(volume, weight, stride, padding):
    kernel = jnp.transpose(weight, (0, 4, 1, 2, 3)).astype(jnp.float32)
    result = lax.conv_general_dilated(volume.astype(jnp.float32)[None], kernel, (stride, stride, stride), padding, dimension_numbers=("NCDHW", "OIDHW", "NCDHW"), precision=lax.Precision.HIGHEST, preferred_element_type=jnp.float32)
    return result[0]


def layer(hidden, probe, weight, bias, weight_probe, stride, padding):
    preact = convolve(hidden, weight, stride, padding) + bias[:, None, None, None]
    change = convolve(hidden, weight_probe, stride, padding)
    if probe is not None:
        change = change + convolve(probe, weight, stride, padding)
    return preact, change


def reference(density, conv1_weight, conv1_bias, conv1_probe, conv2_weight, conv2_bias, conv2_probe, lift_weight, lift_bias, lift_probe, conv3_weight, conv3_bias, conv3_probe):
    preact, change = layer(density, None, conv1_weight, conv1_bias, conv1_probe, 1, "SAME")
    hidden, probe = swish_pair(preact, change)
    hidden = hidden.astype(jnp.bfloat16)
    probe = probe.astype(jnp.bfloat16)
    preact, change = layer(hidden, probe, conv2_weight, conv2_bias, conv2_probe, 1, "SAME")
    hidden, probe = swish_pair(preact, change)
    hidden = hidden.astype(jnp.bfloat16)
    probe = probe.astype(jnp.bfloat16)
    preact, change = layer(hidden, probe, lift_weight, lift_bias, lift_probe, 4, "VALID")
    hidden, probe = swish_pair(preact, change)
    hidden = hidden.astype(jnp.bfloat16)
    probe = probe.astype(jnp.bfloat16)
    preact, change = layer(hidden, probe, conv3_weight, conv3_bias, conv3_probe, 1, "SAME")
    return preact.astype(jnp.bfloat16), change.astype(jnp.bfloat16)
```

```python
import jax
import jax.numpy as jnp
from jax import lax
from jax.experimental import pallas as pl
from jax.experimental.pallas import tpu as pltpu
from jax.sharding import PartitionSpec as P

BF = jnp.bfloat16
F32 = jnp.float32
VM = pl.BlockSpec(memory_space=pltpu.VMEM)
SM = pl.BlockSpec(memory_space=pltpu.SMEM)


def call(kernel, outs, scratch=(), specs=None, flops=1000000):
    return pl.pallas_call(
        kernel,
        out_shape=outs,
        in_specs=specs,
        out_specs=jax.tree.map(lambda _: VM, outs),
        scratch_shapes=list(scratch),
        cost_estimate=pl.CostEstimate(flops=flops, bytes_accessed=100000, transcendentals=0),
    )


def silu_pair(v, direction):
    s = 1.0 / (1.0 + jnp.exp(-v))
    return v * s, s * (1.0 + v * (1.0 - s)) * direction


def iota(shape, dim):
    return lax.broadcasted_iota(jnp.int32, shape, dim)


def pack_kernel(dens, own, to_right, to_left):
    total = jnp.zeros((64, 64), F32)
    for c in range(4):
        rows = dens[c].astype(F32).reshape(64, 16).astype(BF)
        place = (iota((16, 64), 1) == 4 * iota((16, 64), 0) + c).astype(BF)
        total += jnp.dot(rows, place, preferred_element_type=F32)
    own[...] = total.astype(BF)
    for ref, at in ((to_right, 32), (to_left, 0)):
        ref[...] = jnp.concatenate(
            [total[16 * g : 16 * g + 16, at : at + 32] for g in range(4)], axis=1
        ).astype(BF)


SIDES = [(dx, dy) for dx in (-1, 0, 1) for dy in (-1, 0, 1) if dx or dy]


def inside(dx, dy):
    sx, sy = lax.axis_index("sx") + dx, lax.axis_index("sy") + dy
    ok = (sx >= 0) & (sx < 4) & (sy >= 0) & (sy < 8)
    return ok, jnp.where(ok, sx * 8 + sy, 0)


def face_kernel(own, left, right, block, slots, wide):
    def unpack(ref):
        v = ref[...].astype(F32)
        return jnp.concatenate([v[:, 32 * g : 32 * g + 32] for g in range(4)], axis=0)

    cells = jnp.concatenate([unpack(left), own[...].astype(F32), unpack(right)], axis=1)
    block[...] = cells.astype(BF)
    wide[...] = jnp.zeros_like(wide)
    for dx, dy in SIDES:
        ok, at = inside(dx, dy)

        @pl.when(ok)
        def _(dx=dx, dy=dy, at=at):
            xs = range(8) if dx == 0 else ((6, 7) if dx > 0 else (0, 1))
            for j, x in enumerate(xs):
                if dy == 0:
                    wide[at, 8 * j : 8 * j + 8, :] = cells[8 * x : 8 * x + 8]
                else:
                    y = 6 if dy > 0 else 0
                    wide[at, 2 * j : 2 * j + 2, :] = cells[8 * x + y : 8 * x + y + 2]

    slots[...] = wide[...].astype(BF)


def lift_kernel(
    block, slots, t1, b1, t2, b2, lift_w, lift_p, b3, out, dens, win, acc1, hp, acc2, lhs, got
):
    dens[...] = jnp.zeros_like(dens)
    got[...] = slots[...].astype(F32)
    cells = block[...].astype(F32)
    for x in range(8):
        dens[2 + x, 2:10, :] = cells[8 * x : 8 * x + 8]
    for dx, dy in SIDES:
        ok, at = inside(dx, dy)

        @pl.when(ok)
        def _(dx=dx, dy=dy, at=at):
            xs = range(2, 10) if dx == 0 else ((10, 11) if dx > 0 else (0, 1))
            for j, x in enumerate(xs):
                if dy == 0:
                    dens[x, 2:10, :] = got[at, 8 * j : 8 * j + 8, :]
                else:
                    y = 10 if dy > 0 else 0
                    dens[x, y : y + 2, :] = got[at, 2 * j : 2 * j + 2, :]

    lane = iota((8, 128), 1)

    def windows(x, carry):
        shifted = []
        for y in range(12):
            row = jnp.broadcast_to(dens[x, y : y + 1, :], (8, 128))
            first = pltpu.roll(row, 8, 1, stride=16, stride_axis=0)
            shifted.append((first, pltpu.roll(first, 32, 1), pltpu.roll(first, 64, 1)))
        for y in range(10):
            win[x, 8 * y : 8 * y + 8, :] = jnp.where(
                lane < 32, shifted[y][0], jnp.where(lane < 64, shifted[y + 1][1], shifted[y + 2][2])
            )
        return carry

    lax.fori_loop(0, 12, windows, 0)

    rows = jnp.concatenate(
        [win[p : p + 10].reshape(800, 128).astype(BF) for p in range(3)], axis=1
    )
    acc1[...] = jnp.dot(rows, t1[...], preferred_element_type=F32)

    fine = 16 * lax.axis_index("sz") + 4 * (6 - iota((8, 256), 0)) - 1 + iota((8, 256), 1) // 32
    zmask = jnp.where((fine >= 0) & (fine < 256), 1.0, 0.0)
    bias1 = jnp.concatenate([b1[...]] * 6 + [jnp.zeros((1, 64), F32)], axis=1)

    def first(x, carry):
        gx = 8 * lax.axis_index("sx") + x - 1
        okx = (gx >= 0) & (gx < 32)
        for y in range(10):
            gy = 8 * lax.axis_index("sy") + y - 1
            ok = okx & (gy >= 0) & (gy < 64)
            mask = jnp.where(ok, zmask, 0.0)
            at = pl.ds(pl.multiple_of(80 * x + 8 * y, 8), 8)
            h, d = silu_pair(acc1[at, 0:256] + bias1, acc1[at, 256:512])
            hp[x, y] = jnp.concatenate([h * mask, d * mask], axis=0).astype(BF)
        return carry

    lax.fori_loop(0, 10, first, 0)

    for t in range(9):
        p, q = divmod(t, 3)
        part = lax.dot_general(
            hp[p : p + 8, q : q + 8].reshape(1024, 256),
            t2[t],
            (((1,), (1,)), ((), ())),
            preferred_element_type=F32,
        )
        if t == 0:
            acc2[...] = part
        else:
            acc2[...] += part

    bias2 = jnp.concatenate([b2[...]] * 4, axis=1)
    for x in range(8):
        for y in range(8):
            r = 16 * (8 * x + y)
            h, d = silu_pair(
                acc2[r : r + 8, 0:128] + bias2,
                acc2[r : r + 8, 128:256] + acc2[r + 8 : r + 16, 0:128],
            )
            at = 16 * (2 * (x // 4) + y // 4)
            tap = 128 * (4 * (x % 4) + y % 4)
            lhs[at : at + 16, tap : tap + 128] = jnp.concatenate([h, d], axis=0).astype(BF)

    left = lhs[...]
    by_w = jnp.dot(left, lift_w[...], preferred_element_type=F32)
    by_p = jnp.dot(left, lift_p[...], preferred_element_type=F32)
    level = 7 - iota((8, 256), 0)
    coarse = 4 * lax.axis_index("sz") + level - 1
    mask = jnp.where((level < 6) & (coarse >= 0) & (coarse < 64), 1.0, 0.0)
    hs, ds = [], []
    for k in range(4):
        h, d = silu_pair(
            by_w[16 * k : 16 * k + 8] + b3[...],
            by_p[16 * k : 16 * k + 8] + by_w[16 * k + 8 : 16 * k + 16],
        )
        hs.append(h * mask)
        ds.append(d * mask)
    turned = jnp.concatenate(hs + ds, axis=0).T
    for m in range(16):
        chunk = jnp.concatenate(
            [turned[16 * m : 16 * m + 8], turned[16 * m + 8 : 16 * m + 16]], axis=1
        ).astype(BF)
        out[2 * m] = chunk
        out[2 * m + 1] = chunk


def last_kernel(got, w_own, p_own, w_far, p_far, out, flat, turned):
    flat[...] = got[...].astype(F32).reshape(256, 128)
    for c in range(8):
        turned[pl.ds(c, 128, stride=8), 0:32] = flat[pl.ds(c, 32, stride=8), :].T
    lane = iota((8, 128), 1)
    cx, cy, bx, by = lane >> 6, (lane >> 5) & 1, (lane >> 3) & 3, lane & 7

    def shift_x(v, by_one):
        if by_one == 0:
            return v
        if by_one > 0:
            s = jnp.where(cx == 0, pltpu.roll(v, 64, 1), pltpu.roll(v, 56, 1))
            return jnp.where((cx == 1) & (bx == 3), 0.0, s)
        s = jnp.where(cx == 1, pltpu.roll(v, 64, 1), pltpu.roll(v, 72, 1))
        return jnp.where((cx == 0) & (bx == 0), 0.0, s)

    def shift_y(v, by_one):
        if by_one == 0:
            return v
        if by_one > 0:
            s = jnp.where(cy == 0, pltpu.roll(v, 96, 1), pltpu.roll(v, 31, 1))
            return jnp.where((cy == 1) & (by == 7), 0.0, s)
        s = jnp.where(cy == 1, pltpu.roll(v, 32, 1), pltpu.roll(v, 97, 1))
        return jnp.where((cy == 0) & (by == 0), 0.0, s)

    def columns(k, kind):
        pieces = {}
        for z in range(6):
            tile = jnp.concatenate(
                [
                    turned[pl.ds(8 * (64 * k + 32 * kind + 8 * xy + 7 - z), 8), 0:32]
                    for xy in range(4)
                ],
                axis=1,
            )
            for p in range(3):
                moved = shift_x(tile, p - 1)
                for q in range(3):
                    pieces[p, q, z] = shift_y(moved, q - 1)
        return jnp.concatenate(
            [
                jnp.concatenate([pieces[p, q, r + z] for z in range(4)], axis=1)
                for p in range(3)
                for q in range(3)
                for r in range(3)
            ],
            axis=0,
        ).astype(BF)

    core = lax.axis_index("sy") % 2
    first = core == 0

    def pick(a, b):
        return jnp.where(first, a[...], b[...])

    def product(w, x):
        return lax.dot_general(w, x, (((0,), (0,)), ((), ())), preferred_element_type=F32)

    pre, dot = 0.0, 0.0
    for k in range(2):
        w = pick(w_own, w_far) if k == 0 else pick(w_far, w_own)
        d = pick(p_own, p_far) if k == 0 else pick(p_far, p_own)
        h_cols = columns(k, 0)
        pre = pre + product(w, h_cols)
        dot = dot + product(d, h_cols) + product(w, columns(k, 1))
    pre = pre.reshape(16, 2, 8, 512)
    dot = dot.reshape(16, 2, 8, 512)
    pre = jnp.where(first, pre[:, 0], pre[:, 1])
    dot = jnp.where(first, dot[:, 0], dot[:, 1])
    out[...] = jnp.concatenate([pre, dot], axis=1).astype(BF)


def sum_kernel(got, bias, features, tangent, rows):
    total = got[0].astype(F32)
    for s in range(1, 16):
        total = total + got[s].astype(F32)
    level = iota((16, 512), 0)
    for o in range(8):
        total = total + jnp.where(level == o, bias[o], 0.0)
    total = total.astype(BF)
    here, there = iota((128, 128), 0), iota((128, 128), 1)
    gx = 2 * ((here >> 3) & 3) + (here >> 6)
    gy = 2 * (here & 7) + ((here >> 5) & 1)
    place = (there == 16 * gx + gy).astype(BF)
    for z in range(4):
        rows[pl.ds(z, 16, stride=4), :] = jnp.dot(
            total[:, 128 * z : 128 * z + 128], place, preferred_element_type=F32
        )
    for x in range(8):
        moved = rows[...] if x == 0 else pltpu.roll(rows[...], 128 - 16 * x, 1)
        for o in range(8):
            features[o, x] = moved[4 * o : 4 * o + 4, 0:16].astype(BF)
            tangent[o, x] = moved[32 + 4 * o : 32 + 4 * o + 4, 0:16].astype(BF)


def first_matrix(w, p):
    def bands(v):
        v = jnp.transpose(v, (1, 2, 3, 4, 0)).reshape(3, 3, 12, 32)
        wide = [jnp.pad(v, ((0, 0), (0, 0), (4 * z, 20 - 4 * z), (0, 0))) for z in range(6)]
        return jnp.concatenate(wide + [jnp.zeros((3, 3, 32, 64), BF)], axis=3)

    both = jnp.concatenate([bands(w), bands(p)], axis=3).reshape(3, 96, 512)
    return jnp.pad(both, ((0, 0), (0, 32), (0, 0))).reshape(384, 512)


def second_matrix(w, p):
    def bands(v):
        v = jnp.transpose(v, (1, 2, 0, 3, 4)).reshape(9, 32, 96)
        wide = [jnp.pad(v, ((0, 0), (0, 0), (32 * z, 160 - 32 * z))) for z in range(4)]
        return jnp.concatenate(wide, axis=1)

    return jnp.concatenate([bands(w), bands(p)], axis=1)


def body(
    density,
    conv1_weight,
    conv1_bias,
    conv1_probe,
    conv2_weight,
    conv2_bias,
    conv2_probe,
    lift_weight,
    lift_bias,
    lift_probe,
    conv3_weight,
    conv3_bias,
    conv3_probe,
):
    S = jax.ShapeDtypeStruct
    own, to_right, to_left = call(
        pack_kernel, (S((64, 64), BF), S((16, 128), BF), S((16, 128), BF)), specs=[VM]
    )(density)
    from_left = lax.ppermute(to_right, "sz", [(i, i + 1) for i in range(15)])
    from_right = lax.ppermute(to_left, "sz", [(i + 1, i) for i in range(15)])

    def flat3(v):
        return jnp.transpose(v, (1, 2, 3, 4, 0)).reshape(216, 256)

    w3, p3 = flat3(conv3_weight), flat3(conv3_probe)
    swap = [(i, i ^ 1) for i in range(8)]
    w3_far, p3_far = lax.ppermute(w3, "sy", swap), lax.ppermute(p3, "sy", swap)
    t1 = first_matrix(conv1_weight, conv1_probe)
    t2 = second_matrix(conv2_weight, conv2_probe)

    block, slots = call(
        face_kernel,
        (S((64, 128), BF), S((32, 16, 128), BF)),
        scratch=[pltpu.VMEM((32, 16, 128), F32)],
        specs=[VM] * 3,
    )(own, from_left, from_right)
    near = lax.all_to_all(slots, ("sx", "sy"), 0, 0, tiled=True)

    def flat_lift(v):
        return jnp.transpose(v, (1, 2, 3, 4, 0)).reshape(2048, 256)

    lifted = call(
        lift_kernel,
        S((32, 8, 128), BF),
        scratch=[
            pltpu.VMEM((12, 16, 128), F32),
            pltpu.VMEM((12, 80, 128), F32),
            pltpu.VMEM((800, 512), F32),
            pltpu.VMEM((10, 10, 16, 256), BF),
            pltpu.VMEM((1024, 256), F32),
            pltpu.VMEM((64, 2048), BF),
            pltpu.VMEM((32, 16, 128), F32),
        ],
        specs=[VM] * 9,
        flops=10000000,
    )(
        block,
        near,
        t1,
        conv1_bias.reshape(1, 32),
        t2,
        conv2_bias.reshape(1, 32),
        flat_lift(lift_weight),
        flat_lift(lift_probe),
        lift_bias.reshape(1, 256),
    )
    gathered = lax.all_to_all(lifted, ("sx", "sy"), 0, 0, tiled=True)
    parts = call(
        last_kernel,
        S((16, 16, 512), BF),
        scratch=[pltpu.VMEM((256, 128), F32), pltpu.VMEM((1024, 128), F32)],
        specs=[VM] * 5,
        flops=10000000,
    )(gathered, w3, p3, w3_far, p3_far)
    same_core = [[8 * x + 2 * z + c for x in range(4) for z in range(4)] for c in range(2)]
    mine = lax.all_to_all(
        parts, ("sx", "sy"), 0, 0, axis_index_groups=same_core, tiled=True
    )
    features, tangent = call(
        sum_kernel,
        (S((8, 8, 4, 16), BF), S((8, 8, 4, 16), BF)),
        scratch=[pltpu.VMEM((64, 128), F32)],
        specs=[VM, SM],
    )(mine, conv3_bias)
    return jnp.transpose(features, (0, 1, 3, 2)), jnp.transpose(tangent, (0, 1, 3, 2))


def solution(mesh):
    placed = (
        P(None, "sx", "sy", "sz"),
        P(),
        P(),
        P(),
        P(),
        P(),
        P(),
        P(),
        P(),
        P(),
        P(None, None, None, None, ("sx", "sy")),
        P(("sx", "sy")),
        P(None, None, None, None, ("sx", "sy")),
    )
    return jax.shard_map(
        body,
        mesh=mesh,
        in_specs=placed,
        out_specs=(P(("sx", "sy"), None, None, "sz"), P(("sx", "sy"), None, None, "sz")),
        check_vma=False,
    )
```

```python
import jax
import jax.numpy as jnp
from jax import lax
from jax.experimental import pallas as pl
from jax.experimental.pallas import tpu as pltpu
from jax.sharding import PartitionSpec as P


BF = jnp.bfloat16
F32 = jnp.float32
VM = pl.BlockSpec(memory_space=pltpu.VMEM)
SM = pl.BlockSpec(memory_space=pltpu.SMEM)


def call(kernel, outs, scratch=(), specs=None, flops=1000000, mib=4):
    return pl.pallas_call(
        kernel,
        out_shape=outs,
        in_specs=specs,
        out_specs=jax.tree.map(lambda _: VM, outs),
        scratch_shapes=list(scratch),
        cost_estimate=pl.CostEstimate(flops=flops, bytes_accessed=100000, transcendentals=0),
        compiler_params=pltpu.CompilerParams(vmem_limit_bytes=mib << 20),
    )


def silu_pair(v, direction):
    s = 1.0 / (1.0 + jnp.exp(-v))
    return v * s, s * (1.0 + v * (1.0 - s)) * direction


def iota(shape, dim):
    return lax.broadcasted_iota(jnp.int32, shape, dim)


SIDES = [(dx, dy) for dx in (-1, 0, 1) for dy in (-1, 0, 1) if dx or dy]


def inside(dx, dy):
    sx, sy = lax.axis_index("sx") + dx, lax.axis_index("sy") + dy
    ok = (sx >= 0) & (sx < 4) & (sy >= 0) & (sy < 8)
    return ok, jnp.where(ok, sx * 8 + sy, 0)


def face_kernel(dens, own, slots, cells):
    total = jnp.zeros((64, 64), F32)
    for c in range(4):
        rows = dens[c].astype(F32).reshape(64, 16).astype(BF)
        place = (iota((16, 64), 1) == 4 * iota((16, 64), 0) + c).astype(BF)
        total += jnp.dot(rows, place, preferred_element_type=F32)
    own[...] = total.astype(BF)
    cells[...] = jnp.concatenate([total, total], axis=1)
    slots[...] = jnp.zeros_like(slots)
    low = iota((8, 128), 1) < 64
    for dx, dy in SIDES:
        ok, at = inside(dx, dy)

        @pl.when(ok)
        def _(dx=dx, dy=dy, at=at):
            x, y = (6 if dx > 0 else 0), (6 if dy > 0 else 0)
            if dx == 0:
                near, far = cells[pl.ds(y, 8, stride=8), :], cells[pl.ds(y + 1, 8, stride=8), :]
            else:
                near, far = cells[8 * x : 8 * x + 8, :], cells[8 * x + 8 : 8 * x + 16, :]
            slots[at] = jnp.where(low, near, far).astype(BF)


def tile_kernel(own, slots, tile, to_right, to_left, dens):
    dens[...] = jnp.zeros_like(dens)
    cells = own[...].astype(F32)
    for x in range(8):
        dens[2 + x, 2:10, :] = cells[8 * x : 8 * x + 8]
    for dx, dy in SIDES:
        ok, at = inside(dx, dy)

        @pl.when(ok)
        def _(dx=dx, dy=dy, at=at):
            got = slots[at].astype(F32)
            x, y = (10 if dx > 0 else 0), (10 if dy > 0 else 0)
            for j in range(2):
                half = got[:, 64 * j : 64 * j + 64]
                if dx == 0:
                    for i in range(8):
                        dens[2 + i, y + j : y + j + 1, :] = half[i : i + 1]
                elif dy == 0:
                    dens[x + j, 2:10, :] = half
                else:
                    row = 0 if dy > 0 else 6
                    dens[x + j, y : y + 2, :] = half[row : row + 2]

    rows = dens[...].reshape(192, 64)
    tile[...] = rows.astype(BF)
    for ref, at in ((to_right, 32), (to_left, 0)):
        ref[...] = jnp.concatenate(
            [rows[48 * g : 48 * g + 48, at : at + 32] for g in range(4)], axis=1
        ).astype(BF)


def lift_kernel(
    tile, right, left, t1, w2, lift_w, lift_p, biases, out, dens, win, acc1, hp, t2, acc2, lhs
):
    def unpack(ref):
        v = ref[...].astype(F32)
        return jnp.concatenate([v[:, 32 * g : 32 * g + 32] for g in range(4)], axis=0)

    dens[...] = jnp.concatenate(
        [unpack(left), tile[...].astype(F32), unpack(right)], axis=1
    ).reshape(12, 16, 128)
    wide = iota((32, 128), 1)
    for t in range(9):
        for i in range(2):
            v = w2[t, 32 * i : 32 * i + 32].astype(F32)
            for z in range(4):
                moved = v if z == 0 else pltpu.roll(v, 32 * z, 1)
                at = slice(128 * i + 32 * z, 128 * i + 32 * z + 32)
                t2[t, at, 0:128] = jnp.where(wide >= 32 * z, moved, 0.0).astype(BF)
                t2[t, at, 128:256] = jnp.where(wide < 32 * z, moved, 0.0).astype(BF)

    lane = iota((8, 128), 1)

    def windows(x, carry):
        shifted = []
        for y in range(12):
            row = jnp.broadcast_to(dens[x, y : y + 1, :], (8, 128))
            first = pltpu.roll(row, 8, 1, stride=16, stride_axis=0)
            shifted.append((first, pltpu.roll(first, 32, 1), pltpu.roll(first, 64, 1)))
        for y in range(10):
            win[x, 8 * y : 8 * y + 8, :] = jnp.where(
                lane < 32, shifted[y][0], jnp.where(lane < 64, shifted[y + 1][1], shifted[y + 2][2])
            )
        return carry

    lax.fori_loop(0, 12, windows, 0)

    rows = jnp.concatenate(
        [win[p : p + 10].reshape(800, 128).astype(BF) for p in range(3)], axis=1
    )
    acc1[...] = jnp.dot(rows, t1[...], preferred_element_type=F32)

    fine = 16 * lax.axis_index("sz") + 4 * (6 - iota((8, 256), 0)) - 1 + iota((8, 256), 1) // 32
    zmask = jnp.where((fine >= 0) & (fine < 256), 1.0, 0.0)
    bias3, bias1, bias2 = biases[:, 0:256], biases[:, 256:512], biases[:, 512:640]

    def first(x, carry):
        gx = 8 * lax.axis_index("sx") + x - 1
        okx = (gx >= 0) & (gx < 32)
        for y in range(10):
            gy = 8 * lax.axis_index("sy") + y - 1
            ok = okx & (gy >= 0) & (gy < 64)
            mask = jnp.where(ok, zmask, 0.0)
            at = pl.ds(pl.multiple_of(80 * x + 8 * y, 8), 8)
            h, d = silu_pair(acc1[at, 0:256] + bias1, acc1[at, 256:512])
            hp[x, y] = jnp.concatenate([h * mask, d * mask], axis=0).astype(BF)
        return carry

    lax.fori_loop(0, 10, first, 0)

    for t in range(9):
        p, q = divmod(t, 3)
        part = lax.dot_general(
            hp[p : p + 8, q : q + 8].reshape(1024, 256),
            t2[t],
            (((1,), (1,)), ((), ())),
            preferred_element_type=F32,
        )
        if t == 0:
            acc2[...] = part
        else:
            acc2[...] += part

    for x in range(8):
        for y in range(8):
            r = 16 * (8 * x + y)
            h, d = silu_pair(
                acc2[r : r + 8, 0:128] + bias2,
                acc2[r : r + 8, 128:256] + acc2[r + 8 : r + 16, 0:128],
            )
            at = 16 * (2 * (x // 4) + y // 4)
            tap = 128 * (4 * (x % 4) + y % 4)
            lhs[at : at + 16, tap : tap + 128] = jnp.concatenate([h, d], axis=0).astype(BF)

    taps = lhs[...]
    by_w = jnp.dot(taps, lift_w[...], preferred_element_type=F32)
    by_p = jnp.dot(taps, lift_p[...], preferred_element_type=F32)
    level = 7 - iota((8, 256), 0)
    coarse = 4 * lax.axis_index("sz") + level - 1
    mask = jnp.where((level < 6) & (coarse >= 0) & (coarse < 64), 1.0, 0.0)
    hs, ds = [], []
    for k in range(4):
        h, d = silu_pair(
            by_w[16 * k : 16 * k + 8] + bias3,
            by_p[16 * k : 16 * k + 8] + by_w[16 * k + 8 : 16 * k + 16],
        )
        hs.append(h * mask)
        ds.append(d * mask)
    turned = jnp.concatenate(hs + ds, axis=0).T
    for d in range(32):
        four = [turned[8 * (d % 8 + 8 * t) : 8 * (d % 8 + 8 * t) + 8] for t in range(4)]
        out[d] = jnp.concatenate(
            [jnp.concatenate(four[0::2], axis=0), jnp.concatenate(four[1::2], axis=0)], axis=1
        ).astype(BF)


def share_kernel(w, p, out):
    for x in range(4):
        at = slice(64 * x, 64 * x + 64)
        out[x] = jnp.concatenate([w[:, at].astype(F32), p[:, at].astype(F32)], axis=1).astype(BF)


def last_kernel(got, weights, out, flat, turned, pre, dot):
    for g in range(2):
        flat[g] = got[:, 8 * g : 8 * g + 8, :].astype(F32).reshape(256, 128)
        for c in range(8):
            turned[g, pl.ds(c, 128, stride=8), 0:32] = flat[g, pl.ds(c, 32, stride=8), :].T
    lane = iota((8, 128), 1)
    cx, cy, bx, by = lane >> 6, (lane >> 5) & 1, (lane >> 3) & 3, lane & 7

    def shift_x(v, by_one):
        if by_one == 0:
            return v
        if by_one > 0:
            s = jnp.where(cx == 0, pltpu.roll(v, 64, 1), pltpu.roll(v, 56, 1))
            return jnp.where((cx == 1) & (bx == 3), 0.0, s)
        s = jnp.where(cx == 1, pltpu.roll(v, 64, 1), pltpu.roll(v, 72, 1))
        return jnp.where((cx == 0) & (bx == 0), 0.0, s)

    def shift_y(v, by_one):
        if by_one == 0:
            return v
        if by_one > 0:
            s = jnp.where(cy == 0, pltpu.roll(v, 96, 1), pltpu.roll(v, 31, 1))
            return jnp.where((cy == 1) & (by == 7), 0.0, s)
        s = jnp.where(cy == 1, pltpu.roll(v, 32, 1), pltpu.roll(v, 97, 1))
        return jnp.where((cy == 0) & (by == 0), 0.0, s)

    def columns(k, kind):
        pieces = {}
        for z in range(6):
            tile = jnp.concatenate(
                [
                    turned[k // 2, pl.ds(pl.multiple_of(512 * (k % 2) + 8 * (32 * kind + 8 * xy + 7 - z), 8), 8), 0:32]
                    for xy in range(4)
                ],
                axis=1,
            )
            for p in range(3):
                moved = shift_x(tile, p - 1)
                for q in range(3):
                    pieces[p, q, z] = shift_y(moved, q - 1)
        return jnp.concatenate(
            [
                jnp.concatenate([pieces[p, q, r + z] for z in range(4)], axis=1)
                for p in range(3)
                for q in range(3)
                for r in range(3)
            ],
            axis=0,
        ).astype(BF)

    def product(w, x):
        return lax.dot_general(w, x, (((0,), (0,)), ((), ())), preferred_element_type=F32)

    pre[...] = jnp.zeros_like(pre)
    dot[...] = jnp.zeros_like(dot)

    def add(k, carry):
        by_h = product(weights[k], columns(k, 0))
        pre[...] += by_h[0:64]
        dot[...] += by_h[64:128] + product(weights[k], columns(k, 1))[0:64]
        return carry

    lax.fori_loop(0, 4, add, 0)
    out[...] = jnp.concatenate(
        [pre[...].reshape(8, 8, 512), dot[...].reshape(8, 8, 512)], axis=1
    ).astype(BF)


def sum_kernel(got, bias, features, tangent, rows):
    total = got[0].astype(F32)
    for s in range(1, 8):
        total = total + got[s].astype(F32)
    level = iota((16, 512), 0)
    for o in range(8):
        total = total + jnp.where(level == o, bias[o], 0.0)
    total = total.astype(BF)
    here, there = iota((128, 128), 0), iota((128, 128), 1)
    gx = 2 * ((here >> 3) & 3) + (here >> 6)
    gy = 2 * (here & 7) + ((here >> 5) & 1)
    place = (there == 16 * gx + gy).astype(BF)
    for z in range(4):
        rows[pl.ds(z, 16, stride=4), :] = jnp.dot(
            total[:, 128 * z : 128 * z + 128], place, preferred_element_type=F32
        )
    for x in range(8):
        moved = rows[...] if x == 0 else pltpu.roll(rows[...], 128 - 16 * x, 1)
        for o in range(8):
            features[o, x] = moved[4 * o : 4 * o + 4, 0:16].astype(BF)
            tangent[o, x] = moved[32 + 4 * o : 32 + 4 * o + 4, 0:16].astype(BF)


def first_matrix(w, p):
    def bands(v):
        v = jnp.transpose(v, (1, 2, 3, 4, 0)).reshape(3, 3, 12, 32)
        wide = [jnp.pad(v, ((0, 0), (0, 0), (4 * z, 20 - 4 * z), (0, 0))) for z in range(6)]
        return jnp.concatenate(wide + [jnp.zeros((3, 3, 32, 64), BF)], axis=3)

    both = jnp.concatenate([bands(w), bands(p)], axis=3).reshape(3, 96, 512)
    return jnp.pad(both, ((0, 0), (0, 32), (0, 0))).reshape(384, 512)


def second_rows(w, p):
    def rows(v):
        return jnp.pad(jnp.transpose(v, (1, 2, 0, 3, 4)).reshape(9, 32, 96), ((0, 0), (0, 0), (0, 32)))

    return jnp.concatenate([rows(w), rows(p)], axis=1)


def body(
    density,
    conv1_weight,
    conv1_bias,
    conv1_probe,
    conv2_weight,
    conv2_bias,
    conv2_probe,
    lift_weight,
    lift_bias,
    lift_probe,
    conv3_weight,
    conv3_bias,
    conv3_probe,
):
    S = jax.ShapeDtypeStruct
    own, faces = call(
        face_kernel,
        (S((64, 64), BF), S((32, 8, 128), BF)),
        scratch=[pltpu.VMEM((64, 128), F32)],
        specs=[VM],
    )(density)
    near = lax.all_to_all(faces, ("sx", "sy"), 0, 0, tiled=True)
    tile, to_right, to_left = call(
        tile_kernel,
        (S((192, 64), BF), S((48, 128), BF), S((48, 128), BF)),
        scratch=[pltpu.VMEM((12, 16, 64), F32)],
        specs=[VM, VM],
    )(own, near)
    from_right = lax.ppermute(to_left, "sz", [(i + 1, i) for i in range(15)])
    from_left = lax.ppermute(to_right, "sz", [(i, i + 1) for i in range(15)])

    def flat3(v):
        return jnp.transpose(v, (1, 2, 3, 4, 0)).reshape(216, 256)

    share = call(share_kernel, S((4, 216, 128), BF), specs=[VM, VM])(
        flat3(conv3_weight), flat3(conv3_probe)
    )
    shares = lax.all_to_all(share, "sx", 0, 0, tiled=True)
    t1 = first_matrix(conv1_weight, conv1_probe)
    w2 = second_rows(conv2_weight, conv2_probe)

    biases = jnp.concatenate(
        [lift_bias] + [conv1_bias] * 6 + [jnp.zeros(64, F32)] + [conv2_bias] * 4
    ).reshape(1, 640)

    def flat_lift(v):
        return jnp.transpose(v, (1, 2, 3, 4, 0)).reshape(2048, 256)

    lift = call(
        lift_kernel,
        S((32, 16, 128), BF),
        scratch=[
            pltpu.VMEM((12, 16, 128), F32),
            pltpu.VMEM((12, 80, 128), F32),
            pltpu.VMEM((800, 512), F32),
            pltpu.VMEM((10, 10, 16, 256), BF),
            pltpu.VMEM((9, 256, 256), BF),
            pltpu.VMEM((1024, 256), F32),
            pltpu.VMEM((64, 2048), BF),
        ],
        specs=[VM] * 8,
        flops=10000000,
        mib=24,
    )
    lifted = lift(
        tile,
        from_right,
        from_left,
        t1,
        w2,
        flat_lift(lift_weight),
        flat_lift(lift_probe),
        biases,
    )
    gathered = lax.all_to_all(lifted, ("sx", "sy"), 0, 0, tiled=True)
    parts = call(
        last_kernel,
        S((8, 16, 512), BF),
        scratch=[
            pltpu.VMEM((2, 256, 128), F32),
            pltpu.VMEM((2, 1024, 128), F32),
            pltpu.VMEM((64, 512), F32),
            pltpu.VMEM((64, 512), F32),
        ],
        specs=[VM] * 2,
        flops=10000000,
        mib=16,
    )(gathered, shares)
    mine = lax.all_to_all(parts, "sy", 0, 0, tiled=True)
    features, tangent = call(
        sum_kernel,
        (S((8, 8, 4, 16), BF), S((8, 8, 4, 16), BF)),
        scratch=[pltpu.VMEM((64, 128), F32)],
        specs=[VM, SM],
    )(mine, conv3_bias)
    return jnp.transpose(features, (0, 1, 3, 2)), jnp.transpose(tangent, (0, 1, 3, 2))


def solution(mesh):
    placed = (
        P(None, "sx", "sy", "sz"),
        P(),
        P(),
        P(),
        P(),
        P(),
        P(),
        P(),
        P(),
        P(),
        P(None, None, None, None, ("sx", "sy")),
        P(("sx", "sy")),
        P(None, None, None, None, ("sx", "sy")),
    )

    return jax.shard_map(
        body,
        mesh=mesh,
        in_specs=placed,
        out_specs=(P(("sx", "sy"), None, None, "sz"), P(("sx", "sy"), None, None, "sz")),
        check_vma=False,
    )
```

```python
import jax
import jax.numpy as jnp
from jax import lax
from jax.experimental import pallas as pl
from jax.experimental.pallas import tpu as pltpu
from jax.sharding import PartitionSpec as P


BF = jnp.bfloat16
F32 = jnp.float32
VM = pl.BlockSpec(memory_space=pltpu.VMEM)
SM = pl.BlockSpec(memory_space=pltpu.SMEM)


def call(kernel, outs, scratch=(), specs=None, flops=1000000, mib=4):
    return pl.pallas_call(
        kernel,
        out_shape=outs,
        in_specs=specs,
        out_specs=jax.tree.map(lambda _: VM, outs),
        scratch_shapes=list(scratch),
        cost_estimate=pl.CostEstimate(flops=flops, bytes_accessed=100000, transcendentals=0),
        compiler_params=pltpu.CompilerParams(vmem_limit_bytes=mib << 20),
    )


def silu_pair(v, direction):
    s = 1.0 / (1.0 + jnp.exp(-v))
    return v * s, s * (1.0 + v * (1.0 - s)) * direction


def iota(shape, dim):
    return lax.broadcasted_iota(jnp.int32, shape, dim)


SIDES = [(dx, dy) for dx in (-1, 0, 1) for dy in (-1, 0, 1) if dx or dy]


def inside(dx, dy):
    sx, sy = lax.axis_index("sx") + dx, lax.axis_index("sy") + dy
    ok = (sx >= 0) & (sx < 4) & (sy >= 0) & (sy < 8)
    return ok, jnp.where(ok, sx * 8 + sy, 0)


def face_kernel(dens, own, slots, cells):
    total = jnp.zeros((64, 64), F32)
    for c in range(4):
        rows = dens[c].astype(F32).reshape(64, 16).astype(BF)
        place = (iota((16, 64), 1) == 4 * iota((16, 64), 0) + c).astype(BF)
        total += jnp.dot(rows, place, preferred_element_type=F32)
    own[...] = total.astype(BF)
    cells[...] = jnp.concatenate([total, total], axis=1)
    slots[...] = jnp.zeros_like(slots)
    low = iota((8, 128), 1) < 64
    for dx, dy in SIDES:
        ok, at = inside(dx, dy)

        @pl.when(ok)
        def _(dx=dx, dy=dy, at=at):
            x, y = (6 if dx > 0 else 0), (6 if dy > 0 else 0)
            if dx == 0:
                near, far = cells[pl.ds(y, 8, stride=8), :], cells[pl.ds(y + 1, 8, stride=8), :]
            else:
                near, far = cells[8 * x : 8 * x + 8, :], cells[8 * x + 8 : 8 * x + 16, :]
            slots[at] = jnp.where(low, near, far).astype(BF)


def tile_kernel(own, slots, tile, to_right, to_left, dens):
    dens[...] = jnp.zeros_like(dens)
    cells = own[...].astype(F32)
    for x in range(8):
        dens[2 + x, 2:10, :] = cells[8 * x : 8 * x + 8]
    for dx, dy in SIDES:
        ok, at = inside(dx, dy)

        @pl.when(ok)
        def _(dx=dx, dy=dy, at=at):
            got = slots[at].astype(F32)
            x, y = (10 if dx > 0 else 0), (10 if dy > 0 else 0)
            for j in range(2):
                half = got[:, 64 * j : 64 * j + 64]
                if dx == 0:
                    for i in range(8):
                        dens[2 + i, y + j : y + j + 1, :] = half[i : i + 1]
                elif dy == 0:
                    dens[x + j, 2:10, :] = half
                else:
                    row = 0 if dy > 0 else 6
                    dens[x + j, y : y + 2, :] = half[row : row + 2]

    rows = dens[...].reshape(192, 64)
    tile[...] = rows.astype(BF)
    for ref, at in ((to_right, 32), (to_left, 0)):
        ref[...] = jnp.concatenate(
            [rows[48 * g : 48 * g + 48, at : at + 32] for g in range(4)], axis=1
        ).astype(BF)


def lift_kernel(
    tile, right, left, t1, w2, lift_w, lift_p, biases, out, dens, win, acc1, hp, t2, acc2, lhs
):
    def unpack(ref):
        v = ref[...].astype(F32)
        return jnp.concatenate([v[:, 32 * g : 32 * g + 32] for g in range(4)], axis=0)

    dens[...] = jnp.concatenate(
        [unpack(left), tile[...].astype(F32), unpack(right)], axis=1
    ).reshape(12, 16, 128)
    wide = iota((32, 128), 1)
    for t in range(9):
        for i in range(2):
            v = w2[t, 32 * i : 32 * i + 32].astype(F32)
            for z in range(4):
                moved = v if z == 0 else pltpu.roll(v, 32 * z, 1)
                at = slice(128 * i + 32 * z, 128 * i + 32 * z + 32)
                t2[at, 256 * t : 256 * t + 128] = jnp.where(wide >= 32 * z, moved, 0.0).astype(BF)
                t2[at, 256 * t + 128 : 256 * t + 256] = jnp.where(wide < 32 * z, moved, 0.0).astype(BF)

    lane = iota((8, 128), 1)

    def windows(x, carry):
        shifted = []
        for y in range(12):
            row = jnp.broadcast_to(dens[x, y : y + 1, :], (8, 128))
            first = pltpu.roll(row, 8, 1, stride=16, stride_axis=0)
            shifted.append((first, pltpu.roll(first, 32, 1), pltpu.roll(first, 64, 1)))
        for y in range(10):
            win[x, 8 * y : 8 * y + 8, :] = jnp.where(
                lane < 32, shifted[y][0], jnp.where(lane < 64, shifted[y + 1][1], shifted[y + 2][2])
            )
        return carry

    lax.fori_loop(0, 12, windows, 0, unroll=True)

    rows = jnp.concatenate(
        [win[p : p + 10].reshape(800, 128).astype(BF) for p in range(3)], axis=1
    )
    acc1[...] = jnp.dot(rows, t1[...], preferred_element_type=F32)

    fine = 16 * lax.axis_index("sz") + 4 * (6 - iota((8, 256), 0)) - 1 + iota((8, 256), 1) // 32
    zmask = jnp.where((fine >= 0) & (fine < 256), 1.0, 0.0)
    bias3, bias1, bias2 = biases[:, 0:256], biases[:, 256:512], biases[:, 512:640]

    def first(x, carry):
        gx = 8 * lax.axis_index("sx") + x - 1
        okx = (gx >= 0) & (gx < 32)
        for y in range(10):
            gy = 8 * lax.axis_index("sy") + y - 1
            ok = okx & (gy >= 0) & (gy < 64)
            mask = jnp.where(ok, zmask, 0.0)
            at = pl.ds(pl.multiple_of(80 * x + 8 * y, 8), 8)
            h, d = silu_pair(acc1[at, 0:256] + bias1, acc1[at, 256:512])
            hp[x, y] = jnp.concatenate([h * mask, d * mask], axis=0).astype(BF)
        return carry

    lax.fori_loop(0, 10, first, 0, unroll=2)

    for c in range(2):
        rows = jnp.concatenate(
            [
                hp[4 * c + t // 3 : 4 * c + t // 3 + 4, t % 3 : t % 3 + 8].reshape(512, 256)
                for t in range(9)
            ],
            axis=1,
        )
        acc2[512 * c : 512 * c + 512] = lax.dot_general(
            rows, t2[...], (((1,), (1,)), ((), ())), preferred_element_type=F32
        )

    for x in range(8):
        for y in range(8):
            r = 16 * (8 * x + y)
            h, d = silu_pair(
                acc2[r : r + 8, 0:128] + bias2,
                acc2[r : r + 8, 128:256] + acc2[r + 8 : r + 16, 0:128],
            )
            at = 16 * (2 * (x // 4) + y // 4)
            tap = 128 * (4 * (x % 4) + y % 4)
            lhs[at : at + 16, tap : tap + 128] = jnp.concatenate([h, d], axis=0).astype(BF)

    taps = lhs[...]
    by_w = jnp.dot(taps, lift_w[...], preferred_element_type=F32)
    by_p = jnp.dot(taps, lift_p[...], preferred_element_type=F32)
    level = 7 - iota((8, 256), 0)
    coarse = 4 * lax.axis_index("sz") + level - 1
    mask = jnp.where((level < 6) & (coarse >= 0) & (coarse < 64), 1.0, 0.0)
    hs, ds = [], []
    for k in range(4):
        h, d = silu_pair(
            by_w[16 * k : 16 * k + 8] + bias3,
            by_p[16 * k : 16 * k + 8] + by_w[16 * k + 8 : 16 * k + 16],
        )
        hs.append(h * mask)
        ds.append(d * mask)
    turned = jnp.concatenate(hs + ds, axis=0).T
    for d in range(32):
        four = [turned[8 * (d % 8 + 8 * t) : 8 * (d % 8 + 8 * t) + 8] for t in range(4)]
        out[d] = jnp.concatenate(
            [jnp.concatenate(four[0::2], axis=0), jnp.concatenate(four[1::2], axis=0)], axis=1
        ).astype(BF)


def share_kernel(w, p, out):
    for x in range(4):
        at = slice(64 * x, 64 * x + 64)
        out[x] = jnp.concatenate([w[:, at].astype(F32), p[:, at].astype(F32)], axis=1).astype(BF)


def last_kernel(got, weights, out, flat, turned, pre, dot):
    for g in range(2):
        flat[g] = got[:, 8 * g : 8 * g + 8, :].astype(F32).reshape(256, 128)
        for c in range(8):
            turned[g, pl.ds(c, 128, stride=8), 0:32] = flat[g, pl.ds(c, 32, stride=8), :].T
    lane = iota((8, 128), 1)
    cx, cy, bx, by = lane >> 6, (lane >> 5) & 1, (lane >> 3) & 3, lane & 7

    def shift_x(v, by_one):
        if by_one == 0:
            return v
        if by_one > 0:
            s = jnp.where(cx == 0, pltpu.roll(v, 64, 1), pltpu.roll(v, 56, 1))
            return jnp.where((cx == 1) & (bx == 3), 0.0, s)
        s = jnp.where(cx == 1, pltpu.roll(v, 64, 1), pltpu.roll(v, 72, 1))
        return jnp.where((cx == 0) & (bx == 0), 0.0, s)

    def shift_y(v, by_one):
        if by_one == 0:
            return v
        if by_one > 0:
            s = jnp.where(cy == 0, pltpu.roll(v, 96, 1), pltpu.roll(v, 31, 1))
            return jnp.where((cy == 1) & (by == 7), 0.0, s)
        s = jnp.where(cy == 1, pltpu.roll(v, 32, 1), pltpu.roll(v, 97, 1))
        return jnp.where((cy == 0) & (by == 0), 0.0, s)

    def columns(k, kind):
        pieces = {}
        for z in range(6):
            tile = jnp.concatenate(
                [
                    turned[k // 2, pl.ds(pl.multiple_of(512 * (k % 2) + 8 * (32 * kind + 8 * xy + 7 - z), 8), 8), 0:32]
                    for xy in range(4)
                ],
                axis=1,
            )
            for p in range(3):
                moved = shift_x(tile, p - 1)
                for q in range(3):
                    pieces[p, q, z] = shift_y(moved, q - 1)
        return jnp.concatenate(
            [
                jnp.concatenate([pieces[p, q, r + z] for z in range(4)], axis=1)
                for p in range(3)
                for q in range(3)
                for r in range(3)
            ],
            axis=0,
        ).astype(BF)

    def product(w, x):
        return lax.dot_general(w, x, (((0,), (0,)), ((), ())), preferred_element_type=F32)

    pre[...] = jnp.zeros_like(pre)
    dot[...] = jnp.zeros_like(dot)

    def add(k, carry):
        by_h = product(weights[k], columns(k, 0))
        pre[...] += by_h[0:64]
        dot[...] += by_h[64:128] + product(weights[k], columns(k, 1))[0:64]
        return carry

    lax.fori_loop(0, 4, add, 0)
    out[...] = jnp.concatenate(
        [pre[...].reshape(8, 8, 512), dot[...].reshape(8, 8, 512)], axis=1
    ).astype(BF)


def sum_kernel(got, bias, features, tangent, rows):
    total = got[0].astype(F32)
    for s in range(1, 8):
        total = total + got[s].astype(F32)
    level = iota((16, 512), 0)
    for o in range(8):
        total = total + jnp.where(level == o, bias[o], 0.0)
    total = total.astype(BF)
    here, there = iota((128, 128), 0), iota((128, 128), 1)
    gx = 2 * ((here >> 3) & 3) + (here >> 6)
    gy = 2 * (here & 7) + ((here >> 5) & 1)
    place = (there == 16 * gx + gy).astype(BF)
    for z in range(4):
        rows[pl.ds(z, 16, stride=4), :] = jnp.dot(
            total[:, 128 * z : 128 * z + 128], place, preferred_element_type=F32
        )
    for x in range(8):
        moved = rows[...] if x == 0 else pltpu.roll(rows[...], 128 - 16 * x, 1)
        for o in range(8):
            features[o, x] = moved[4 * o : 4 * o + 4, 0:16].astype(BF)
            tangent[o, x] = moved[32 + 4 * o : 32 + 4 * o + 4, 0:16].astype(BF)


def first_matrix(w, p):
    def bands(v):
        v = jnp.transpose(v, (1, 2, 3, 4, 0)).reshape(3, 3, 12, 32)
        wide = [jnp.pad(v, ((0, 0), (0, 0), (4 * z, 20 - 4 * z), (0, 0))) for z in range(6)]
        return jnp.concatenate(wide + [jnp.zeros((3, 3, 32, 64), BF)], axis=3)

    both = jnp.concatenate([bands(w), bands(p)], axis=3).reshape(3, 96, 512)
    return jnp.pad(both, ((0, 0), (0, 32), (0, 0))).reshape(384, 512)


def second_rows(w, p):
    def rows(v):
        return jnp.pad(jnp.transpose(v, (1, 2, 0, 3, 4)).reshape(9, 32, 96), ((0, 0), (0, 0), (0, 32)))

    return jnp.concatenate([rows(w), rows(p)], axis=1)


def body(
    density,
    conv1_weight,
    conv1_bias,
    conv1_probe,
    conv2_weight,
    conv2_bias,
    conv2_probe,
    lift_weight,
    lift_bias,
    lift_probe,
    conv3_weight,
    conv3_bias,
    conv3_probe,
):
    S = jax.ShapeDtypeStruct
    own, faces = call(
        face_kernel,
        (S((64, 64), BF), S((32, 8, 128), BF)),
        scratch=[pltpu.VMEM((64, 128), F32)],
        specs=[VM],
    )(density)
    near = lax.all_to_all(faces, ("sx", "sy"), 0, 0, tiled=True)
    tile, to_right, to_left = call(
        tile_kernel,
        (S((192, 64), BF), S((48, 128), BF), S((48, 128), BF)),
        scratch=[pltpu.VMEM((12, 16, 64), F32)],
        specs=[VM, VM],
    )(own, near)
    from_right = lax.ppermute(to_left, "sz", [(i + 1, i) for i in range(15)])
    from_left = lax.ppermute(to_right, "sz", [(i, i + 1) for i in range(15)])

    def flat3(v):
        return jnp.transpose(v, (1, 2, 3, 4, 0)).reshape(216, 256)

    share = call(share_kernel, S((4, 216, 128), BF), specs=[VM, VM])(
        flat3(conv3_weight), flat3(conv3_probe)
    )
    shares = lax.all_to_all(share, "sx", 0, 0, tiled=True)
    t1 = first_matrix(conv1_weight, conv1_probe)
    w2 = second_rows(conv2_weight, conv2_probe)

    biases = jnp.concatenate(
        [lift_bias] + [conv1_bias] * 6 + [jnp.zeros(64, F32)] + [conv2_bias] * 4
    ).reshape(1, 640)

    def flat_lift(v):
        return jnp.transpose(v, (1, 2, 3, 4, 0)).reshape(2048, 256)

    lift = call(
        lift_kernel,
        S((32, 16, 128), BF),
        scratch=[
            pltpu.VMEM((12, 16, 128), F32),
            pltpu.VMEM((12, 80, 128), F32),
            pltpu.VMEM((800, 512), F32),
            pltpu.VMEM((10, 10, 16, 256), BF),
            pltpu.VMEM((256, 2304), BF),
            pltpu.VMEM((1024, 256), F32),
            pltpu.VMEM((64, 2048), BF),
        ],
        specs=[VM] * 8,
        flops=10000000,
        mib=24,
    )
    lifted = lift(
        tile,
        from_right,
        from_left,
        t1,
        w2,
        flat_lift(lift_weight),
        flat_lift(lift_probe),
        biases,
    )
    gathered = lax.all_to_all(lifted, ("sx", "sy"), 0, 0, tiled=True)
    parts = call(
        last_kernel,
        S((8, 16, 512), BF),
        scratch=[
            pltpu.VMEM((2, 256, 128), F32),
            pltpu.VMEM((2, 1024, 128), F32),
            pltpu.VMEM((64, 512), F32),
            pltpu.VMEM((64, 512), F32),
        ],
        specs=[VM] * 2,
        flops=10000000,
        mib=16,
    )(gathered, shares)
    mine = lax.all_to_all(parts, "sy", 0, 0, tiled=True)
    features, tangent = call(
        sum_kernel,
        (S((8, 8, 4, 16), BF), S((8, 8, 4, 16), BF)),
        scratch=[pltpu.VMEM((64, 128), F32)],
        specs=[VM, SM],
    )(mine, conv3_bias)
    return jnp.transpose(features, (0, 1, 3, 2)), jnp.transpose(tangent, (0, 1, 3, 2))


def solution(mesh):
    placed = (
        P(None, "sx", "sy", "sz"),
        P(),
        P(),
        P(),
        P(),
        P(),
        P(),
        P(),
        P(),
        P(),
        P(None, None, None, None, ("sx", "sy")),
        P(("sx", "sy")),
        P(None, None, None, None, ("sx", "sy")),
    )

    return jax.shard_map(
        body,
        mesh=mesh,
        in_specs=placed,
        out_specs=(P(("sx", "sy"), None, None, "sz"), P(("sx", "sy"), None, None, "sz")),
        check_vma=False,
    )
```

```python
import jax
import jax.numpy as jnp
from jax import lax
from jax.experimental import pallas as pl
from jax.experimental.pallas import tpu as pltpu
from jax.sharding import PartitionSpec as P


BF = jnp.bfloat16
F32 = jnp.float32
VM = pl.BlockSpec(memory_space=pltpu.VMEM)
SM = pl.BlockSpec(memory_space=pltpu.SMEM)


def call(kernel, outs, scratch=(), specs=None, flops=1000000, mib=4):
    return pl.pallas_call(
        kernel,
        out_shape=outs,
        in_specs=specs,
        out_specs=jax.tree.map(lambda _: VM, outs),
        scratch_shapes=list(scratch),
        cost_estimate=pl.CostEstimate(flops=flops, bytes_accessed=100000, transcendentals=0),
        compiler_params=pltpu.CompilerParams(vmem_limit_bytes=mib << 20),
    )


def silu_pair(v, direction):
    s = 1.0 / (1.0 + jnp.exp(-v))
    return v * s, s * (1.0 + v * (1.0 - s)) * direction


def iota(shape, dim):
    return lax.broadcasted_iota(jnp.int32, shape, dim)


SIDES = [(dx, dy) for dx in (-1, 0, 1) for dy in (-1, 0, 1) if dx or dy]


def inside(dx, dy):
    sx, sy = lax.axis_index("sx") + dx, lax.axis_index("sy") + dy
    ok = (sx >= 0) & (sx < 4) & (sy >= 0) & (sy < 8)
    return ok, jnp.where(ok, sx * 8 + sy, 0)


def face_kernel(dens, own, slots, cells):
    total = jnp.zeros((64, 64), F32)
    for c in range(4):
        rows = dens[c].astype(F32).reshape(64, 16).astype(BF)
        place = (iota((16, 64), 1) == 4 * iota((16, 64), 0) + c).astype(BF)
        total += jnp.dot(rows, place, preferred_element_type=F32)
    own[...] = total.astype(BF)
    cells[...] = jnp.concatenate([total, total], axis=1)
    slots[...] = jnp.zeros_like(slots)
    low = iota((8, 128), 1) < 64
    for dx, dy in SIDES:
        ok, at = inside(dx, dy)

        @pl.when(ok)
        def _(dx=dx, dy=dy, at=at):
            x, y = (6 if dx > 0 else 0), (6 if dy > 0 else 0)
            if dx == 0:
                near, far = cells[pl.ds(y, 8, stride=8), :], cells[pl.ds(y + 1, 8, stride=8), :]
            else:
                near, far = cells[8 * x : 8 * x + 8, :], cells[8 * x + 8 : 8 * x + 16, :]
            slots[at] = jnp.where(low, near, far).astype(BF)


def tile_kernel(own, slots, tile, to_right, to_left, dens):
    dens[...] = jnp.zeros_like(dens)
    cells = own[...].astype(F32)
    for x in range(8):
        dens[2 + x, 2:10, :] = cells[8 * x : 8 * x + 8]
    for dx, dy in SIDES:
        ok, at = inside(dx, dy)

        @pl.when(ok)
        def _(dx=dx, dy=dy, at=at):
            got = slots[at].astype(F32)
            x, y = (10 if dx > 0 else 0), (10 if dy > 0 else 0)
            for j in range(2):
                half = got[:, 64 * j : 64 * j + 64]
                if dx == 0:
                    for i in range(8):
                        dens[2 + i, y + j : y + j + 1, :] = half[i : i + 1]
                elif dy == 0:
                    dens[x + j, 2:10, :] = half
                else:
                    row = 0 if dy > 0 else 6
                    dens[x + j, y : y + 2, :] = half[row : row + 2]

    rows = dens[...].reshape(192, 64)
    tile[...] = rows.astype(BF)
    for ref, at in ((to_right, 32), (to_left, 0)):
        ref[...] = jnp.concatenate(
            [rows[48 * g : 48 * g + 48, at : at + 32] for g in range(4)], axis=1
        ).astype(BF)


def lift_kernel(
    tile, right, left, t1, w2, p2, lift_w, lift_p, biases, out, dens, win, acc1, hp, t2, acc2, lhs
):
    def unpack(ref):
        v = ref[...].astype(F32)
        return jnp.concatenate([v[:, 32 * g : 32 * g + 32] for g in range(4)], axis=0)

    dens[...] = jnp.concatenate(
        [unpack(left), tile[...].astype(F32), unpack(right)], axis=1
    ).reshape(12, 16, 128)
    wide = iota((32, 128), 1)
    for t in range(9):
        for i in range(2):
            ref = (w2, p2)[i]
            v = jnp.concatenate(
                [ref[3 * t + r].astype(F32) for r in range(3)] + [jnp.zeros((32, 32), F32)], axis=1
            )
            for z in range(4):
                moved = v if z == 0 else pltpu.roll(v, 32 * z, 1)
                at = slice(128 * i + 32 * z, 128 * i + 32 * z + 32)
                t2[at, 256 * t : 256 * t + 128] = jnp.where(wide >= 32 * z, moved, 0.0).astype(BF)
                t2[at, 256 * t + 128 : 256 * t + 256] = jnp.where(wide < 32 * z, moved, 0.0).astype(BF)

    lane = iota((8, 128), 1)

    def windows(x, carry):
        shifted = []
        for y in range(12):
            row = jnp.broadcast_to(dens[x, y : y + 1, :], (8, 128))
            first = pltpu.roll(row, 8, 1, stride=16, stride_axis=0)
            shifted.append((first, pltpu.roll(first, 32, 1), pltpu.roll(first, 64, 1)))
        for y in range(10):
            win[x, 8 * y : 8 * y + 8, :] = jnp.where(
                lane < 32, shifted[y][0], jnp.where(lane < 64, shifted[y + 1][1], shifted[y + 2][2])
            )
        return carry

    lax.fori_loop(0, 12, windows, 0, unroll=True)

    rows = jnp.concatenate(
        [win[p : p + 10].reshape(800, 128).astype(BF) for p in range(3)], axis=1
    )
    acc1[...] = jnp.dot(rows, t1[...], preferred_element_type=F32)

    fine = 16 * lax.axis_index("sz") + 4 * (6 - iota((8, 256), 0)) - 1 + iota((8, 256), 1) // 32
    zmask = jnp.where((fine >= 0) & (fine < 256), 1.0, 0.0)
    bias3, bias1, bias2 = biases[:, 0:256], biases[:, 256:512], biases[:, 512:640]

    def first(x, carry):
        gx = 8 * lax.axis_index("sx") + x - 1
        okx = (gx >= 0) & (gx < 32)
        for y in range(10):
            gy = 8 * lax.axis_index("sy") + y - 1
            ok = okx & (gy >= 0) & (gy < 64)
            mask = jnp.where(ok, zmask, 0.0)
            at = pl.ds(pl.multiple_of(80 * x + 8 * y, 8), 8)
            h, d = silu_pair(acc1[at, 0:256] + bias1, acc1[at, 256:512])
            hp[x, y] = jnp.concatenate([h * mask, d * mask], axis=0).astype(BF)
        return carry

    lax.fori_loop(0, 10, first, 0, unroll=2)

    for c in range(2):
        rows = jnp.concatenate(
            [
                hp[4 * c + t // 3 : 4 * c + t // 3 + 4, t % 3 : t % 3 + 8].reshape(512, 256)
                for t in range(9)
            ],
            axis=1,
        )
        acc2[512 * c : 512 * c + 512] = lax.dot_general(
            rows, t2[...], (((1,), (1,)), ((), ())), preferred_element_type=F32
        )

    for x in range(8):
        for y in range(8):
            r = 16 * (8 * x + y)
            h, d = silu_pair(
                acc2[r : r + 8, 0:128] + bias2,
                acc2[r : r + 8, 128:256] + acc2[r + 8 : r + 16, 0:128],
            )
            at = 16 * (2 * (x // 4) + y // 4)
            tap = 128 * (4 * (x % 4) + y % 4)
            lhs[at : at + 16, tap : tap + 128] = jnp.concatenate([h, d], axis=0).astype(BF)

    taps = lhs[...]
    by_w = jnp.dot(taps, lift_w[...], preferred_element_type=F32)
    by_p = jnp.dot(taps, lift_p[...], preferred_element_type=F32)
    level = 7 - iota((8, 256), 0)
    coarse = 4 * lax.axis_index("sz") + level - 1
    mask = jnp.where((level < 6) & (coarse >= 0) & (coarse < 64), 1.0, 0.0)
    hs, ds = [], []
    for k in range(4):
        h, d = silu_pair(
            by_w[16 * k : 16 * k + 8] + bias3,
            by_p[16 * k : 16 * k + 8] + by_w[16 * k + 8 : 16 * k + 16],
        )
        hs.append(h * mask)
        ds.append(d * mask)
    turned = jnp.concatenate(hs + ds, axis=0).T
    for d in range(32):
        four = [turned[8 * (d % 8 + 8 * t) : 8 * (d % 8 + 8 * t) + 8] for t in range(4)]
        out[d] = jnp.concatenate(
            [jnp.concatenate(four[0::2], axis=0), jnp.concatenate(four[1::2], axis=0)], axis=1
        ).astype(BF)


def share_kernel(w, p, out):
    for x in range(4):
        at = slice(64 * x, 64 * x + 64)
        out[x] = jnp.concatenate([w[:, at].astype(F32), p[:, at].astype(F32)], axis=1).astype(BF)


def last_kernel(got, weights, out, flat, turned, pre, dot):
    for g in range(2):
        flat[g] = got[:, 8 * g : 8 * g + 8, :].astype(F32).reshape(256, 128)
        for c in range(8):
            turned[g, pl.ds(c, 128, stride=8), 0:32] = flat[g, pl.ds(c, 32, stride=8), :].T
    lane = iota((8, 128), 1)
    cx, cy, bx, by = lane >> 6, (lane >> 5) & 1, (lane >> 3) & 3, lane & 7

    def shift_x(v, by_one):
        if by_one == 0:
            return v
        if by_one > 0:
            s = jnp.where(cx == 0, pltpu.roll(v, 64, 1), pltpu.roll(v, 56, 1))
            return jnp.where((cx == 1) & (bx == 3), 0.0, s)
        s = jnp.where(cx == 1, pltpu.roll(v, 64, 1), pltpu.roll(v, 72, 1))
        return jnp.where((cx == 0) & (bx == 0), 0.0, s)

    def shift_y(v, by_one):
        if by_one == 0:
            return v
        if by_one > 0:
            s = jnp.where(cy == 0, pltpu.roll(v, 96, 1), pltpu.roll(v, 31, 1))
            return jnp.where((cy == 1) & (by == 7), 0.0, s)
        s = jnp.where(cy == 1, pltpu.roll(v, 32, 1), pltpu.roll(v, 97, 1))
        return jnp.where((cy == 0) & (by == 0), 0.0, s)

    def columns(k, kind):
        pieces = {}
        for z in range(6):
            tile = jnp.concatenate(
                [
                    turned[k // 2, pl.ds(pl.multiple_of(512 * (k % 2) + 8 * (32 * kind + 8 * xy + 7 - z), 8), 8), 0:32]
                    for xy in range(4)
                ],
                axis=1,
            )
            for p in range(3):
                moved = shift_x(tile, p - 1)
                for q in range(3):
                    pieces[p, q, z] = shift_y(moved, q - 1)
        return jnp.concatenate(
            [
                jnp.concatenate([pieces[p, q, r + z] for z in range(4)], axis=1)
                for p in range(3)
                for q in range(3)
                for r in range(3)
            ],
            axis=0,
        ).astype(BF)

    def product(w, x):
        return lax.dot_general(w, x, (((0,), (0,)), ((), ())), preferred_element_type=F32)

    pre[...] = jnp.zeros_like(pre)
    dot[...] = jnp.zeros_like(dot)

    def add(k, carry):
        by_h = product(weights[k], columns(k, 0))
        pre[...] += by_h[0:64]
        dot[...] += by_h[64:128] + product(weights[k], columns(k, 1))[0:64]
        return carry

    lax.fori_loop(0, 4, add, 0)
    out[...] = jnp.concatenate(
        [pre[...].reshape(8, 8, 512), dot[...].reshape(8, 8, 512)], axis=1
    ).astype(BF)


def sum_kernel(got, bias, features, tangent, rows):
    total = got[0].astype(F32)
    for s in range(1, 8):
        total = total + got[s].astype(F32)
    level = iota((16, 512), 0)
    for o in range(8):
        total = total + jnp.where(level == o, bias[o], 0.0)
    total = total.astype(BF)
    here, there = iota((128, 128), 0), iota((128, 128), 1)
    gx = 2 * ((here >> 3) & 3) + (here >> 6)
    gy = 2 * (here & 7) + ((here >> 5) & 1)
    place = (there == 16 * gx + gy).astype(BF)
    for z in range(4):
        rows[pl.ds(z, 16, stride=4), :] = jnp.dot(
            total[:, 128 * z : 128 * z + 128], place, preferred_element_type=F32
        )
    for x in range(8):
        moved = rows[...] if x == 0 else pltpu.roll(rows[...], 128 - 16 * x, 1)
        for o in range(8):
            features[o, x] = moved[4 * o : 4 * o + 4, 0:16].astype(BF)
            tangent[o, x] = moved[32 + 4 * o : 32 + 4 * o + 4, 0:16].astype(BF)


def first_matrix(w, p):
    def bands(v):
        v = jnp.transpose(v, (1, 2, 3, 4, 0)).reshape(3, 3, 12, 32)
        wide = [jnp.pad(v, ((0, 0), (0, 0), (4 * z, 20 - 4 * z), (0, 0))) for z in range(6)]
        return jnp.concatenate(wide + [jnp.zeros((3, 3, 32, 64), BF)], axis=3)

    both = jnp.concatenate([bands(w), bands(p)], axis=3).reshape(3, 96, 512)
    return jnp.pad(both, ((0, 0), (0, 32), (0, 0))).reshape(384, 512)


def second_rows(v):
    return jnp.transpose(v, (1, 2, 3, 0, 4)).reshape(27, 32, 32)


def body(
    density,
    conv1_weight,
    conv1_bias,
    conv1_probe,
    conv2_weight,
    conv2_bias,
    conv2_probe,
    lift_weight,
    lift_bias,
    lift_probe,
    conv3_weight,
    conv3_bias,
    conv3_probe,
):
    S = jax.ShapeDtypeStruct
    own, faces = call(
        face_kernel,
        (S((64, 64), BF), S((32, 8, 128), BF)),
        scratch=[pltpu.VMEM((64, 128), F32)],
        specs=[VM],
    )(density)
    near = lax.all_to_all(faces, ("sx", "sy"), 0, 0, tiled=True)
    tile, to_right, to_left = call(
        tile_kernel,
        (S((192, 64), BF), S((48, 128), BF), S((48, 128), BF)),
        scratch=[pltpu.VMEM((12, 16, 64), F32)],
        specs=[VM, VM],
    )(own, near)
    from_right = lax.ppermute(to_left, "sz", [(i + 1, i) for i in range(15)])
    from_left = lax.ppermute(to_right, "sz", [(i, i + 1) for i in range(15)])

    def flat3(v):
        return jnp.transpose(v, (1, 2, 3, 4, 0)).reshape(216, 256)

    share = call(share_kernel, S((4, 216, 128), BF), specs=[VM, VM])(
        flat3(conv3_weight), flat3(conv3_probe)
    )
    shares = lax.all_to_all(share, "sx", 0, 0, tiled=True)
    t1 = first_matrix(conv1_weight, conv1_probe)
    w2, p2 = second_rows(conv2_weight), second_rows(conv2_probe)

    biases = jnp.concatenate(
        [lift_bias] + [conv1_bias] * 6 + [jnp.zeros(64, F32)] + [conv2_bias] * 4
    ).reshape(1, 640)

    def flat_lift(v):
        return jnp.transpose(v, (1, 2, 3, 4, 0)).reshape(2048, 256)

    lift = call(
        lift_kernel,
        S((32, 16, 128), BF),
        scratch=[
            pltpu.VMEM((12, 16, 128), F32),
            pltpu.VMEM((12, 80, 128), F32),
            pltpu.VMEM((800, 512), F32),
            pltpu.VMEM((10, 10, 16, 256), BF),
            pltpu.VMEM((256, 2304), BF),
            pltpu.VMEM((1024, 256), F32),
            pltpu.VMEM((64, 2048), BF),
        ],
        specs=[VM] * 9,
        flops=10000000,
        mib=24,
    )
    lifted = lift(
        tile,
        from_right,
        from_left,
        t1,
        w2,
        p2,
        flat_lift(lift_weight),
        flat_lift(lift_probe),
        biases,
    )
    gathered = lax.all_to_all(lifted, ("sx", "sy"), 0, 0, tiled=True)
    parts = call(
        last_kernel,
        S((8, 16, 512), BF),
        scratch=[
            pltpu.VMEM((2, 256, 128), F32),
            pltpu.VMEM((2, 1024, 128), F32),
            pltpu.VMEM((64, 512), F32),
            pltpu.VMEM((64, 512), F32),
        ],
        specs=[VM] * 2,
        flops=10000000,
        mib=16,
    )(gathered, shares)
    mine = lax.all_to_all(parts, "sy", 0, 0, tiled=True)
    features, tangent = call(
        sum_kernel,
        (S((8, 8, 4, 16), BF), S((8, 8, 4, 16), BF)),
        scratch=[pltpu.VMEM((64, 128), F32)],
        specs=[VM, SM],
    )(mine, conv3_bias)
    return jnp.transpose(features, (0, 1, 3, 2)), jnp.transpose(tangent, (0, 1, 3, 2))


def solution(mesh):
    placed = (
        P(None, "sx", "sy", "sz"),
        P(),
        P(),
        P(),
        P(),
        P(),
        P(),
        P(),
        P(),
        P(),
        P(None, None, None, None, ("sx", "sy")),
        P(("sx", "sy")),
        P(None, None, None, None, ("sx", "sy")),
    )

    return jax.shard_map(
        body,
        mesh=mesh,
        in_specs=placed,
        out_specs=(P(("sx", "sy"), None, None, "sz"), P(("sx", "sy"), None, None, "sz")),
        check_vma=False,
    )
```
